32 devices in a mesh: seq: 4 (over z), exp: 8 (over y, x, core).
Axes of the slice: x: 2, y: 2, z: 4, core: 2. Of those that a mesh axis runs over, the one named last changes fastest.
Arguments:
- queries: bfloat16 [8, 256, 4096], P('exp', 'seq'), may hold values from -30 to 30
- key_heads: bfloat16 [8, 256, 512], P('exp', 'seq'), may hold values from -12 to 12
- value_heads: bfloat16 [8, 256, 512], P('exp', 'seq'), may hold values from -6 to 6
- residual: bfloat16 [8, 256, 4096], P('exp', 'seq'), may hold values from -16 to 16
- lengths: int32 [8, 6], P('exp'), may hold values from 1 to 128, 256 in all within a row
- routes: int32 [8, 256, 4], P('exp', 'seq'), may hold values from 0 to 7, all different within a row; in each aligned block of 64 rows (0 to 63, 64 to 127, ..., all dimensions but the last counted through in order) at most 40 rows name the same one
- gate_weights: bfloat16 [8, 256, 8], P('exp', 'seq'), may hold values from 0.049804688 to 0.29882812
- out_weight: bfloat16 [4096, 4096], P('seq', 'exp'), may hold values from -0.09375 to 0.09375
- norm_gain: float32 [4096], replicated, may hold values from 0.5 to 1.5
- w_gate: bfloat16 [8, 4, 4096, 768], P('exp', 'seq'), may hold values from -0.09375 to 0.09375
- w_up: bfloat16 [8, 4, 4096, 768], P('exp', 'seq'), may hold values from -0.09375 to 0.09375
- w_down: bfloat16 [8, 4, 768, 4096], P('exp', 'seq'), may hold values from -0.15625 to 0.15625
Outputs:
- result: bfloat16 [8, 256, 4096], P('exp', 'seq')
The draws below stay inside these ranges and needn't reach their ends.
Inputs may be any that keep to these rules, and one draw needn't show every extreme that they name: `lengths`: each row sums to 256, and its largest entry is 128. `routes`: the 4 entries of a token differ; among the rows of one device no column is named more than 40 times, a bound that some block reaches.
All inputs are finite; a program needn't handle non-finite values.
Results may differ from the reference program's by a relative error of at most 0.008.
Values may be sent and summed in bfloat16 or wider, within the bound.
A program may use at most 128 MiB of HBM per device.

```python
import math
import jax
import jax.numpy as jnp
import numpy as np
from jax import lax

D = 4096
HQ = 32
KV_HEADS = 4
HEAD_DIM = 128
FF = 1536
EXP_COL = 2
NODES_TOK = 4
EPISODES = 6
TOK_DEV = 64
LENGTH = 256
PACKS = 8
MOST_LEN = 128
CAP = 40
TOP = 8
FF_PART = 768
N_SEQ = 4
N_EXP = 8


def draw_queries(key, part):
    noise_key = jax.random.fold_in(key, 11)
    drawn = jnp.clip(jax.random.normal(noise_key, (PACKS, LENGTH, HQ * HEAD_DIM), jnp.float32), -6.0, 6.0)
    return drawn.astype(jnp.bfloat16)


def draw_key_heads(key, part):
    noise_key = jax.random.fold_in(key, 12)
    drawn = jnp.clip(jax.random.normal(noise_key, (PACKS, LENGTH, KV_HEADS * HEAD_DIM), jnp.float32), -6.0, 6.0)
    return drawn.astype(jnp.bfloat16)


def draw_residual(key, part):
    noise_key = jax.random.fold_in(key, 21)
    drawn = jnp.clip(jax.random.normal(noise_key, (PACKS, LENGTH, D), jnp.float32), -6.0, 6.0)
    return drawn.astype(jnp.bfloat16)


def level_of(rng, dims, pieces, least, largest):
    gain = 1.0
    for dim, parts in pieces:
        heights = jax.random.uniform(jax.random.fold_in(jax.random.fold_in(rng, 6), dim), (parts,), jnp.float32, least / len(pieces), largest / len(pieces))
        gain = gain * jnp.repeat(jnp.exp(heights), dims[dim] // parts).reshape((-1,) + (1,) * (len(dims) - 1 - dim))
    return gain


def length_profile(count, total, reach, skew):
    weights = [(1 << 20) // math.isqrt(standing ** skew) + 1 for standing in range(2, count + 1)]
    surplus, holding = total - reach - (count - 1), [1] * (count - 1)
    while surplus > 0:
        movable = [i for i in range(count - 1) if holding[i] < reach]
        mass, left = sum([weights[i] for i in movable]), surplus
        for i in movable:
            addition = min(reach - holding[i], max(1, left * weights[i] // mass), surplus)
            holding[i] = holding[i] + addition
            surplus = surplus - addition
    return np.array([reach] + holding)


def ragged(own_key, amount, total, reach, skew):
    if amount == 2:
        one = jax.random.randint(own_key, (), max(1, total - reach), min(reach, total - 1) + 1)
        return jnp.stack([one, total - one])
    tallies = jnp.asarray(length_profile(amount, total, reach, skew), jnp.int32)
    twos = (amount - 1) // 2
    source_of, sink = tallies[1:1 + 2 * twos:2], tallies[2:2 + 2 * twos:2]
    room = jnp.minimum(source_of - 1, reach - sink)
    moved = jax.random.randint(jax.random.fold_in(own_key, 1), (twos,), 0, 1 << 20) % (room + 1)
    tallies = tallies.at[1:1 + 2 * twos:2].set(source_of - moved).at[2:2 + 2 * twos:2].set(sink + moved)
    return tallies[jax.random.permutation(jax.random.fold_in(own_key, 2), amount)]


def assign_block(rng, own, number, rows, amount, top, limit, skew):
    order = jax.random.permutation(rng, amount)
    packed, ordinary = shares(amount, rows * top, limit, skew, True), shares(amount, rows * top, limit, skew, False)
    places = jnp.arange(amount)

    def named(sizes, rotation):
        used = int((sizes > 0).sum())
        fixed = max(1, used // 4)
        passed = fixed + (places - fixed + rotation * (used - fixed)) % max(1, amount - fixed)
        return jnp.zeros((amount,), jnp.int32).at[order[jnp.where(places < fixed, places, passed)]].set(jnp.asarray(sizes, jnp.int32))

    sizes = jnp.where(number % 4 == 0, named(packed, number // 4), named(ordinary, number - number // 4 - 1))
    mixed = jax.random.permutation(jax.random.fold_in(own, 3), amount)
    source_of, taker = mixed[0:amount // 2 * 2:2], mixed[1:amount // 2 * 2:2]
    margin = jnp.minimum(sizes[source_of] - 1, limit - sizes[taker]) // 2
    margin = jnp.where((source_of == order[0]) | (taker == order[0]) | (sizes[taker] == 0), 0, jnp.maximum(margin, 0))
    passed = jax.random.randint(jax.random.fold_in(own, 4), (amount // 2,), 0, 1 << 20) % (margin + 1)
    sizes = sizes.at[source_of].add(-passed).at[taker].add(passed)
    members = jnp.searchsorted(jnp.cumsum(sizes), jnp.arange(rows * top), side="right").astype(jnp.int32)
    table = members.reshape(top, rows).T
    table = table[jax.random.permutation(jax.random.fold_in(own, 1), rows)]
    rotation = jax.random.randint(jax.random.fold_in(own, 2), (rows, 1), 0, top)
    return jnp.take_along_axis(table, (jnp.arange(top)[None, :] + rotation) % top, axis=1)


def shares(number_of, total, limit, skew, full):
    portions = [(1 << 20) // math.isqrt(rank ** skew) + 1 for rank in range(1, number_of + 1)]
    largest = limit if full else min(limit, max(-(-total // number_of), total * portions[0] // sum(portions)))
    least = 1 if total - largest >= number_of - 1 else 0
    counts, spare = [largest] + [least] * (number_of - 1), total - largest - least * (number_of - 1)
    while spare > 0:
        free = [i for i in range(1, number_of) if counts[i] < largest] or [i for i in range(1, number_of) if counts[i] < limit]
        whole, left = sum([portions[i] for i in free]), spare
        for i in free:
            addition = min(limit - counts[i], max(1, left * portions[i] // whole), spare)
            counts[i] = counts[i] + addition
            spare = spare - addition
    return np.array(counts)


def bell_draw(rng, extent, scale, limit, cuts=(), kind=jnp.bfloat16):
    drawn = jax.random.normal(rng, extent, jnp.float32) * scale
    if len(cuts) > 0:
        drawn = level_of(rng, extent, cuts, -0.22, 0.18) * drawn
    return jnp.clip(drawn, min=-limit, max=limit).astype(kind)


def setup_inputs(seed: int = 0) -> dict:
    seeds = jax.random.split(jax.random.key(seed), 13)
    queries = draw_queries(jax.random.fold_in(seeds[12], 71), 0)
    key_heads = draw_key_heads(jax.random.fold_in(seeds[12], 71), 0)
    value_heads = bell_draw(seeds[2], (PACKS, LENGTH, KV_HEADS * HEAD_DIM), 1.0, 6.0, ((0, 8), (1, 4)))
    residual = draw_residual(jax.random.fold_in(seeds[12], 71), 0)
    lengths = jax.vmap(lambda own: ragged(own, EPISODES, LENGTH, MOST_LEN, 2))(jax.random.split(seeds[4], PACKS)).reshape((PACKS, EPISODES)).astype(jnp.int32)
    routes_keys = jax.random.split(jax.random.fold_in(seeds[5], 1), PACKS * LENGTH // TOK_DEV)
    routes_turns = jax.random.permutation(jax.random.fold_in(seeds[5], 3), PACKS * LENGTH // TOK_DEV)
    routes = jax.vmap(lambda own, number: assign_block(jax.random.fold_in(seeds[5], 2), own, number, TOK_DEV, N_EXP, NODES_TOK, CAP, 2))(routes_keys, routes_turns).reshape((PACKS, LENGTH, NODES_TOK))
    gate_weights = jnp.clip(0.049804688 + 0.24902344 * jax.random.uniform(seeds[6], (PACKS, LENGTH, TOP), jnp.float32) ** level_of(seeds[6], (PACKS, LENGTH, TOP), ((0, 8), (1, 4)), -0.2, 0.2), 0.049804688, 0.29882812).astype(jnp.bfloat16)
    out_weight = bell_draw(seeds[7], (HQ * HEAD_DIM, D), (HQ * HEAD_DIM) ** -0.5, 0.09375, ((0, 4), (1, 8)))
    norm_gain = jnp.clip(1.0 + 0.1 * jax.random.normal(seeds[8], (D,), jnp.float32), 0.5, 1.5)
    w_gate = bell_draw(seeds[9], (N_EXP, N_SEQ, D, FF_PART), D ** -0.5, 0.09375, ((0, 8), (1, 4)))
    w_up = bell_draw(seeds[10], (N_EXP, N_SEQ, D, FF_PART), D ** -0.5, 0.09375, ((0, 8), (1, 4)))
    w_down = bell_draw(seeds[11], (N_EXP, N_SEQ, FF_PART, D), FF ** -0.5, 0.15625, ((0, 8), (1, 4)))
    return dict(queries=queries, key_heads=key_heads, value_heads=value_heads, residual=residual, lengths=lengths, routes=routes, gate_weights=gate_weights, out_weight=out_weight, norm_gain=norm_gain, w_gate=w_gate, w_up=w_up, w_down=w_down)


epsilon = 1e-06

def episode_ids(length_row, position_count):
    bounds = jnp.cumsum(length_row)
    position = jnp.arange(position_count, dtype=jnp.int32)
    return lax.optimization_barrier(jnp.sum((position[:, None] >= bounds[None, :]).astype(jnp.int32), axis=1))

def attend(query_rows, key_rows, value_rows, episode):
    row_count = query_rows.shape[0]
    groups = key_rows.shape[1] // HEAD_DIM
    per_group = query_rows.shape[1] // HEAD_DIM // groups
    q_heads = query_rows.astype(jnp.float32).reshape(row_count, groups, per_group, HEAD_DIM)
    k_heads = key_rows.astype(jnp.float32).reshape(row_count, groups, HEAD_DIM)
    v_heads = value_rows.astype(jnp.float32).reshape(row_count, groups, HEAD_DIM)
    scores = jnp.einsum('tgpd,ugd->gptu', q_heads, k_heads) / math.sqrt(HEAD_DIM)
    position = jnp.arange(row_count, dtype=jnp.int32)
    allowed = (episode[:, None] == episode[None, :]) & (position[None, :] <= position[:, None])
    scores = jnp.where(allowed, scores, -jnp.inf)
    row_maximum = lax.optimization_barrier(jnp.max(scores, axis=-1, keepdims=True))
    weights = jnp.exp(scores - row_maximum)
    probability = (weights / lax.optimization_barrier(jnp.sum(weights, axis=-1, keepdims=True))).astype(jnp.bfloat16)
    mixed = jnp.einsum('gptu,ugd->tgpd', probability.astype(jnp.float32), v_heads)
    return mixed.astype(jnp.bfloat16).reshape(row_count, groups * per_group * HEAD_DIM)

def reference(queries, key_heads, value_heads, residual, lengths, routes, gate_weights, out_weight, norm_gain, w_gate, w_up, w_down):

    def one_pack(pack_args):
        query_rows, key_rows, value_rows, length_row = pack_args
        return attend(query_rows, key_rows, value_rows, episode_ids(length_row, LENGTH))
    mixed = lax.map(one_pack, (queries, key_heads, value_heads, lengths))
    projected = jnp.dot(mixed.reshape(-1, HQ * HEAD_DIM), out_weight, preferred_element_type=jnp.float32)
    hidden = residual.reshape(-1, D).astype(jnp.float32) + projected
    inverse = lax.rsqrt(lax.optimization_barrier(jnp.mean(hidden * hidden, axis=1, keepdims=True)) + epsilon)
    normalized_rows = (hidden * inverse * norm_gain[None, :]).astype(jnp.bfloat16)
    routed = routes.reshape(-1, NODES_TOK)
    gate_pair = gate_weights.reshape(-1, NODES_TOK, EXP_COL).astype(jnp.float32)
    token_total = routed.shape[0]
    slot_limit = CAP * N_SEQ * N_EXP
    halves = N_SEQ // EXP_COL

    def column(carry_sum, column_id):
        on_node = routed == column_id
        member = jnp.any(on_node, axis=1)
        rank = jnp.cumsum(member.astype(jnp.int32)) - 1
        slot = jnp.where(member, rank, slot_limit)
        row_index = jnp.zeros((slot_limit + 1,), jnp.int32).at[slot].set(jnp.arange(token_total, dtype=jnp.int32))[:slot_limit]
        valid_slot = jnp.zeros((slot_limit + 1,), jnp.float32).at[slot].set(1.0)[:slot_limit]
        token_rows = normalized_rows[row_index]
        node_route_gate = lax.optimization_barrier(jnp.sum(jnp.where(on_node[:, :, None], gate_pair, 0.0), axis=1))[row_index]
        gate_block = w_gate[column_id]
        up_block = w_up[column_id]
        down_block = w_down[column_id]
        accum_sum = jnp.zeros((slot_limit, D), jnp.float32)
        for expert_slot in range(EXP_COL):
            for half_slot in range(halves):
                entry = expert_slot * halves + half_slot
                gate_proj = jnp.dot(token_rows, gate_block[entry], preferred_element_type=jnp.float32)
                up_proj = jnp.dot(token_rows, up_block[entry], preferred_element_type=jnp.float32)
                activated = (jax.nn.silu(gate_proj) * up_proj).astype(jnp.bfloat16)
                partial_value = jnp.dot(activated, down_block[entry], preferred_element_type=jnp.float32).astype(jnp.bfloat16)
                partial_value = lax.optimization_barrier(partial_value)
                weighted = (partial_value.astype(jnp.float32) * node_route_gate[:, expert_slot:expert_slot + 1]).astype(jnp.bfloat16)
                weighted = lax.optimization_barrier(weighted)
                accum_sum = accum_sum + weighted.astype(jnp.float32)
        node_sum = lax.optimization_barrier(accum_sum.astype(jnp.bfloat16))
        node_sum = node_sum.astype(jnp.float32) * valid_slot[:, None]
        return (carry_sum.at[row_index].add(node_sum), None)
    mixture_expert_total, _ = lax.scan(column, jnp.zeros((token_total, D), jnp.float32), jnp.arange(N_EXP, dtype=jnp.int32))
    return (hidden + mixture_expert_total).astype(jnp.bfloat16).reshape(PACKS, LENGTH, D)
```

```python
import math

import jax
import jax.numpy as jnp
from jax import lax
from jax.sharding import PartitionSpec as P

HEAD_DIM = 128
EXP_COL = 2


epsilon = 1e-06


def episode_ids(length_row, position_count):
    bounds = jnp.cumsum(length_row)
    position = jnp.arange(position_count, dtype=jnp.int32)
    return jnp.sum((position[:, None] >= bounds[None, :]).astype(jnp.int32), axis=1)


def attend(query_rows, key_rows, value_rows, episode):
    row_count = query_rows.shape[0]
    groups = key_rows.shape[1] // HEAD_DIM
    per_group = query_rows.shape[1] // HEAD_DIM // groups
    q_heads = query_rows.reshape(row_count, groups, per_group, HEAD_DIM)
    k_heads = key_rows.reshape(row_count, groups, HEAD_DIM)
    v_heads = value_rows.reshape(row_count, groups, HEAD_DIM)
    scores = jnp.einsum(
        "tgpd,ugd->gptu", q_heads, k_heads, preferred_element_type=jnp.float32
    ) / math.sqrt(HEAD_DIM)
    position = jnp.arange(row_count, dtype=jnp.int32)
    allowed = (episode[:, None] == episode[None, :]) & (position[None, :] <= position[:, None])
    scores = jnp.where(allowed, scores, -jnp.inf)
    row_maximum = jnp.max(scores, axis=-1, keepdims=True)
    weights = jnp.exp(scores - row_maximum)
    probability = (weights / jnp.sum(weights, axis=-1, keepdims=True)).astype(jnp.bfloat16)
    mixed = jnp.einsum("gptu,ugd->tgpd", probability, v_heads, preferred_element_type=jnp.float32)
    return mixed.astype(jnp.bfloat16).reshape(row_count, groups * per_group * HEAD_DIM)


def local_routed(
    queries,
    key_heads,
    value_heads,
    residual,
    lengths,
    routes,
    gate_weights,
    out_weight,
    norm_gain,
    w_gate,
    w_up,
    w_down,
):
    seq_count = lax.axis_size("seq")
    columns = lax.axis_size("exp")
    token_count = residual.shape[1]
    model_width = residual.shape[2]
    whole_q, whole_k, whole_v = (
        lax.all_to_all(queries[0], "seq", split_axis=1, concat_axis=0, tiled=True),
        lax.all_to_all(key_heads[0], "seq", split_axis=1, concat_axis=0, tiled=True),
        lax.all_to_all(value_heads[0], "seq", split_axis=1, concat_axis=0, tiled=True),
    )
    episode = episode_ids(lengths[0], whole_q.shape[0])
    mixed = attend(whole_q, whole_k, whole_v, episode)
    head_partial = jnp.dot(
        mixed,
        lax.all_gather(out_weight, "exp", axis=1, tiled=True),
        preferred_element_type=jnp.float32,
    )
    projected = lax.psum_scatter(
        head_partial.astype(jnp.bfloat16), "seq", scatter_dimension=0, tiled=True
    ).astype(jnp.float32)
    hidden = residual[0].astype(jnp.float32) + projected
    inverse = lax.rsqrt(jnp.mean(hidden * hidden, axis=1, keepdims=True) + epsilon)
    normalized_rows = (hidden * inverse * norm_gain[None, :]).astype(jnp.bfloat16)
    routed = routes[0]
    node_count = routed.shape[1]
    capacity = max(2, 5 * token_count * node_count // (4 * columns))
    on_node = routed[:, :, None] == jnp.arange(columns, dtype=jnp.int32)[None, None, :]
    member = jnp.sum(on_node.astype(jnp.int32), axis=1)
    before = jnp.cumsum(member, axis=0) - member
    slot_lookup_index = (
        before[:, :, None] == jnp.arange(capacity, dtype=jnp.int32)[None, None, :]
    ) & (member[:, :, None] > 0)
    slot_flag_mask = slot_lookup_index.astype(jnp.bfloat16)
    outbound = jnp.einsum(
        "roj,rm->ojm", slot_flag_mask, normalized_rows, preferred_element_type=jnp.float32
    ).astype(jnp.bfloat16)
    gate_pair = gate_weights[0].reshape(token_count, node_count, EXP_COL).astype(jnp.float32)
    node_route_gate = jnp.einsum(
        "tnc,tne->tce", on_node.astype(jnp.float32), gate_pair, precision=lax.Precision.HIGHEST
    )
    slot_gate = jnp.einsum(
        "qnr,qny->nry",
        slot_lookup_index.astype(jnp.float32),
        node_route_gate,
        precision=lax.Precision.HIGHEST,
    ).astype(jnp.bfloat16)
    rows_in, gate_in = (
        lax.all_to_all(outbound, "exp", split_axis=0, concat_axis=0, tiled=True),
        lax.all_to_all(slot_gate, "exp", split_axis=0, concat_axis=0, tiled=True),
    )
    rows_all, gate_all = (
        lax.all_gather(rows_in, "seq", axis=0, tiled=True),
        lax.all_gather(gate_in, "seq", axis=0, tiled=True),
    )
    halves = seq_count // EXP_COL
    expert_pick = lax.axis_index("seq") // halves
    flat_rows = rows_all.reshape(-1, model_width)
    flat_gate = lax.dynamic_index_in_dim(
        gate_all.reshape(-1, EXP_COL), expert_pick, axis=1, keepdims=False
    )
    gate_block = w_gate[0, 0]
    up_block = w_up[0, 0]
    down_block = w_down[0, 0]
    gate_proj = jnp.dot(flat_rows, gate_block, preferred_element_type=jnp.float32)
    up_proj = jnp.dot(flat_rows, up_block, preferred_element_type=jnp.float32)
    activated = (jax.nn.silu(gate_proj) * up_proj).astype(jnp.bfloat16)
    partial_value = jnp.dot(activated, down_block, preferred_element_type=jnp.float32).astype(
        jnp.bfloat16
    )
    partial_value = lax.optimization_barrier(partial_value)
    node_sum = lax.psum_scatter(
        (partial_value.astype(jnp.float32) * flat_gate.astype(jnp.float32)[:, None]).astype(
            jnp.bfloat16
        ),
        "seq",
        scatter_dimension=0,
        tiled=True,
    )
    gathered_output = lax.all_to_all(
        node_sum.reshape(columns, capacity, model_width),
        "exp",
        split_axis=0,
        concat_axis=0,
        tiled=True,
    )
    mixture_expert_total = jnp.einsum(
        "gyr,yre->ge", slot_flag_mask, gathered_output, preferred_element_type=jnp.float32
    )
    return (hidden + mixture_expert_total).astype(jnp.bfloat16)[None]

CORE, X_BIT, Y_BIT = 1, 2, 4
CHUNKS = 2


def exchange(value, mask):
    columns = lax.axis_size("exp")
    return lax.ppermute(value, "exp", [(i, i ^ mask) for i in range(columns)])


def shift(value, step):
    seq_count = lax.axis_size("seq")
    return lax.ppermute(value, "seq", [(i, (i + step) % seq_count) for i in range(seq_count)])


def add_rounded(first, second):
    return (first.astype(jnp.float32) + second.astype(jnp.float32)).astype(jnp.bfloat16)


def attend_at(query_rows, key_rows, value_rows, position, length_row):
    row_count = query_rows.shape[0]
    groups = key_rows.shape[1] // HEAD_DIM
    per_group = query_rows.shape[1] // HEAD_DIM // groups
    bounds = jnp.cumsum(length_row)
    episode = jnp.sum((position[:, None] >= bounds[None, :]).astype(jnp.int32), axis=1)
    q_heads = query_rows.reshape(row_count, groups, per_group, HEAD_DIM)
    k_heads = key_rows.reshape(row_count, groups, HEAD_DIM)
    v_heads = value_rows.reshape(row_count, groups, HEAD_DIM)
    scores = jnp.einsum(
        "tgpd,ugd->gptu", q_heads, k_heads, preferred_element_type=jnp.float32
    ) / math.sqrt(HEAD_DIM)
    allowed = (episode[:, None] == episode[None, :]) & (position[None, :] <= position[:, None])
    scores = jnp.where(allowed, scores, -jnp.inf)
    row_maximum = jnp.max(scores, axis=-1, keepdims=True)
    weights = jnp.exp(scores - row_maximum)
    probability = (weights / jnp.sum(weights, axis=-1, keepdims=True)).astype(jnp.bfloat16)
    mixed = jnp.einsum("gptu,ugd->tgpd", probability, v_heads, preferred_element_type=jnp.float32)
    return mixed.astype(jnp.bfloat16).reshape(row_count, groups * per_group * HEAD_DIM)


def project(mixed, out_weight, token_count):
    seq_count = lax.axis_size("seq")
    columns = lax.axis_size("exp")
    width = out_weight.shape[1] // 2
    own = (out_weight[:, :width], out_weight[:, width:])
    pieces = {}
    for half, (first, second) in enumerate(((X_BIT, Y_BIT), (Y_BIT, X_BIT))):
        pieces[half, 0] = own[half]
        pieces[half, first] = exchange(own[half], first)
        pieces[half, second] = exchange(own[half], second)
        pieces[half, first | second] = exchange(pieces[half, first], second)
    for half, m in list(pieces):
        pieces[half, m | CORE] = exchange(pieces[half, m], CORE)
    groups = (
        [(h, m) for h in range(2) for m in (0, 1)],
        [(0, X_BIT), (0, X_BIT | 1), (1, Y_BIT), (1, Y_BIT | 1)],
        [(0, Y_BIT), (0, Y_BIT | 1), (1, X_BIT), (1, X_BIT | 1)],
        [(h, m) for h in range(2) for m in (6, 7)],
    )
    reduced = {}
    for names in groups:
        weight = jnp.concatenate([pieces[name] for name in names], axis=1)
        part = jnp.dot(mixed, weight, preferred_element_type=jnp.float32).astype(jnp.bfloat16)
        total = part[:token_count].astype(jnp.float32)
        for k in range(1, seq_count):
            total = total + shift(part[k * token_count : (k + 1) * token_count], -k).astype(
                jnp.float32
            )
        for place, name in enumerate(names):
            reduced[name] = total[:, place * width : (place + 1) * width]
    halves = [jnp.stack([reduced[h, m] for m in range(columns)]) for h in range(2)]
    here = lax.axis_index("exp")
    in_order = []
    for c in range(columns):
        for h in range(2):
            in_order.append(lax.dynamic_index_in_dim(halves[h], here ^ c, 0, keepdims=False))
    return jnp.concatenate(in_order, axis=1)


def gather_gates(node_gate):
    seq_count = lax.axis_size("seq")
    value = jnp.stack([node_gate] + [shift(node_gate, k) for k in range(1, seq_count)])
    for mask in (X_BIT, Y_BIT, CORE):
        value = jnp.stack([value, exchange(value, mask)])
    pick = lax.axis_index("exp") * EXP_COL + lax.axis_index("seq") // (seq_count // EXP_COL)
    return lax.dynamic_index_in_dim(value, pick, axis=value.ndim - 1, keepdims=False)


def spread(rows):
    seq_count = lax.axis_size("seq")
    blocks = [rows] + [shift(rows, k) for k in range(1, seq_count)]
    near = seq_count // 2
    pieces = []
    for half, (first, second) in enumerate(((X_BIT, Y_BIT), (Y_BIT, X_BIT))):
        own = jnp.concatenate(blocks[half * near : (half + 1) * near], axis=0)
        held = {0: own}
        held[first] = exchange(own, first)
        held[second] = exchange(own, second)
        held[first | second] = exchange(held[first], second)
        pieces += [held[m] for m in (0, X_BIT, Y_BIT, X_BIT | Y_BIT)]
    same = jnp.concatenate(pieces, axis=0)
    return same, exchange(same, CORE)


def collect(same, other, row_count):
    seq_count = lax.axis_size("seq")
    near = seq_count // 2
    summed = add_rounded(same, exchange(other, CORE))
    size = near * row_count
    total = None
    for half, (first, second) in enumerate(((X_BIT, Y_BIT), (Y_BIT, X_BIT))):
        held = {}
        for place, m in enumerate((0, X_BIT, Y_BIT, X_BIT | Y_BIT)):
            start = (4 * half + place) * size
            held[m] = summed[start : start + size]
        onward = add_rounded(held[first], exchange(held[first | second], second))
        mine = held[0].astype(jnp.float32) + exchange(held[second], second).astype(jnp.float32)
        mine = (mine + exchange(onward, first).astype(jnp.float32)).astype(jnp.bfloat16)
        for j in range(near):
            k = half * near + j
            block = mine[j * row_count : (j + 1) * row_count]
            block = block if k == 0 else shift(block, -k)
            block = block.astype(jnp.float32)
            total = block if total is None else total + block
    return total


def expert_part(rows, gate, w_gate, w_up, w_down):
    gate_proj = jnp.dot(rows, w_gate, preferred_element_type=jnp.float32)
    up_proj = jnp.dot(rows, w_up, preferred_element_type=jnp.float32)
    activated = (jax.nn.silu(gate_proj) * up_proj).astype(jnp.bfloat16)
    partial_value = jnp.dot(activated, w_down, preferred_element_type=jnp.float32)
    partial_value = lax.reduce_precision(partial_value, 8, 7)
    return (partial_value * gate[:, None].astype(jnp.float32)).astype(jnp.bfloat16)


def local_dense(
    queries,
    key_heads,
    value_heads,
    residual,
    lengths,
    routes,
    gate_weights,
    out_weight,
    norm_gain,
    w_gate,
    w_up,
    w_down,
):
    seq_count = lax.axis_size("seq")
    columns = lax.axis_size("exp")
    token_count = residual.shape[1]
    place = lax.axis_index("seq")

    def heads_of(k):
        owner = lax.rem(place + k, seq_count)
        parts = []
        for whole in (queries[0], key_heads[0], value_heads[0]):
            width = whole.shape[1] // seq_count
            parts.append(lax.dynamic_slice_in_dim(whole, owner * width, width, axis=1))
        return jnp.concatenate(parts, axis=1)

    arrived = [heads_of(0)] + [shift(heads_of(k), k) for k in range(1, seq_count)]
    rows = jnp.concatenate(arrived, axis=0)
    q_width = queries.shape[2] // seq_count
    k_width = key_heads.shape[2] // seq_count
    position = jnp.concatenate(
        [
            lax.rem(place - k + seq_count, seq_count) * token_count
            + jnp.arange(token_count, dtype=jnp.int32)
            for k in range(seq_count)
        ]
    )
    mixed = attend_at(
        rows[:, :q_width],
        rows[:, q_width : q_width + k_width],
        rows[:, q_width + k_width :],
        position,
        lengths[0],
    )

    routed = routes[0]
    node_count = routed.shape[1]
    on_node = routed[:, :, None] == jnp.arange(columns, dtype=jnp.int32)[None, None, :]
    gate_pair = gate_weights[0].reshape(token_count, node_count, EXP_COL).astype(jnp.float32)
    node_gate = jnp.sum(jnp.where(on_node[:, :, :, None], gate_pair[:, :, None, :], 0.0), axis=1)
    node_gate = node_gate.astype(jnp.bfloat16).reshape(token_count, columns * EXP_COL)
    gates = gather_gates(node_gate)

    hidden = residual[0].astype(jnp.float32) + project(mixed, out_weight, token_count)
    inverse = lax.rsqrt(jnp.mean(hidden * hidden, axis=1, keepdims=True) + epsilon)
    normalized_rows = (hidden * inverse * norm_gain[None, :]).astype(jnp.bfloat16)

    row_count = token_count // CHUNKS
    near = seq_count // 2
    gates = gates.reshape(2, 2, 2, 2, near, CHUNKS, row_count)
    gates = jnp.transpose(gates, (0, 5, 3, 1, 2, 4, 6)).reshape(2, CHUNKS, -1)
    totals = []
    for chunk in range(CHUNKS):
        same, other = spread(normalized_rows[chunk * row_count : (chunk + 1) * row_count])
        weights = (w_gate[0, 0], w_up[0, 0], w_down[0, 0])
        other_out = expert_part(other, gates[1, chunk], *weights)
        same_out = expert_part(same, gates[0, chunk], *weights)
        totals.append(collect(same_out, other_out, row_count))
    return (hidden + jnp.concatenate(totals, axis=0)).astype(jnp.bfloat16)[None]


def solution(mesh):
    cube = (CORE | X_BIT | Y_BIT) + 1
    dense = mesh.shape["exp"] == cube and mesh.shape["seq"] % 2 == 0
    return jax.shard_map(
        local_dense if dense else local_routed,
        mesh=mesh,
        in_specs=(
            P("exp", "seq", None),
            P("exp", "seq", None),
            P("exp", "seq", None),
            P("exp", "seq", None),
            P("exp", None),
            P("exp", "seq", None),
            P("exp", "seq", None),
            P("seq", "exp"),
            P(),
            P("exp", "seq", None, None),
            P("exp", "seq", None, None),
            P("exp", "seq", None, None),
        ),
        out_specs=P("exp", "seq", None),
        check_vma=False,
    )
```

```python
import math

import jax
import jax.numpy as jnp
from jax import lax
from jax.sharding import PartitionSpec as P

HEAD_DIM = 128
EXP_COL = 2


epsilon = 1e-06


def episode_ids(length_row, position_count):
    bounds = jnp.cumsum(length_row)
    position = jnp.arange(position_count, dtype=jnp.int32)
    return jnp.sum((position[:, None] >= bounds[None, :]).astype(jnp.int32), axis=1)


def attend(query_rows, key_rows, value_rows, episode):
    row_count = query_rows.shape[0]
    groups = key_rows.shape[1] // HEAD_DIM
    per_group = query_rows.shape[1] // HEAD_DIM // groups
    q_heads = query_rows.reshape(row_count, groups, per_group, HEAD_DIM)
    k_heads = key_rows.reshape(row_count, groups, HEAD_DIM)
    v_heads = value_rows.reshape(row_count, groups, HEAD_DIM)
    scores = jnp.einsum(
        "tgpd,ugd->gptu", q_heads, k_heads, preferred_element_type=jnp.float32
    ) / math.sqrt(HEAD_DIM)
    position = jnp.arange(row_count, dtype=jnp.int32)
    allowed = (episode[:, None] == episode[None, :]) & (position[None, :] <= position[:, None])
    scores = jnp.where(allowed, scores, -jnp.inf)
    row_maximum = jnp.max(scores, axis=-1, keepdims=True)
    weights = jnp.exp(scores - row_maximum)
    probability = (weights / jnp.sum(weights, axis=-1, keepdims=True)).astype(jnp.bfloat16)
    mixed = jnp.einsum("gptu,ugd->tgpd", probability, v_heads, preferred_element_type=jnp.float32)
    return mixed.astype(jnp.bfloat16).reshape(row_count, groups * per_group * HEAD_DIM)


def local_routed(
    queries,
    key_heads,
    value_heads,
    residual,
    lengths,
    routes,
    gate_weights,
    out_weight,
    norm_gain,
    w_gate,
    w_up,
    w_down,
):
    seq_count = lax.axis_size("seq")
    columns = lax.axis_size("exp")
    token_count = residual.shape[1]
    model_width = residual.shape[2]
    whole_q, whole_k, whole_v = (
        lax.all_to_all(queries[0], "seq", split_axis=1, concat_axis=0, tiled=True),
        lax.all_to_all(key_heads[0], "seq", split_axis=1, concat_axis=0, tiled=True),
        lax.all_to_all(value_heads[0], "seq", split_axis=1, concat_axis=0, tiled=True),
    )
    episode = episode_ids(lengths[0], whole_q.shape[0])
    mixed = attend(whole_q, whole_k, whole_v, episode)
    head_partial = jnp.dot(
        mixed,
        lax.all_gather(out_weight, "exp", axis=1, tiled=True),
        preferred_element_type=jnp.float32,
    )
    projected = lax.psum_scatter(
        head_partial.astype(jnp.bfloat16), "seq", scatter_dimension=0, tiled=True
    ).astype(jnp.float32)
    hidden = residual[0].astype(jnp.float32) + projected
    inverse = lax.rsqrt(jnp.mean(hidden * hidden, axis=1, keepdims=True) + epsilon)
    normalized_rows = (hidden * inverse * norm_gain[None, :]).astype(jnp.bfloat16)
    routed = routes[0]
    node_count = routed.shape[1]
    capacity = max(2, 5 * token_count * node_count // (4 * columns))
    on_node = routed[:, :, None] == jnp.arange(columns, dtype=jnp.int32)[None, None, :]
    member = jnp.sum(on_node.astype(jnp.int32), axis=1)
    before = jnp.cumsum(member, axis=0) - member
    slot_lookup_index = (
        before[:, :, None] == jnp.arange(capacity, dtype=jnp.int32)[None, None, :]
    ) & (member[:, :, None] > 0)
    slot_flag_mask = slot_lookup_index.astype(jnp.bfloat16)
    outbound = jnp.einsum(
        "roj,rm->ojm", slot_flag_mask, normalized_rows, preferred_element_type=jnp.float32
    ).astype(jnp.bfloat16)
    gate_pair = gate_weights[0].reshape(token_count, node_count, EXP_COL).astype(jnp.float32)
    node_route_gate = jnp.einsum(
        "tnc,tne->tce", on_node.astype(jnp.float32), gate_pair, precision=lax.Precision.HIGHEST
    )
    slot_gate = jnp.einsum(
        "qnr,qny->nry",
        slot_lookup_index.astype(jnp.float32),
        node_route_gate,
        precision=lax.Precision.HIGHEST,
    ).astype(jnp.bfloat16)
    rows_in, gate_in = (
        lax.all_to_all(outbound, "exp", split_axis=0, concat_axis=0, tiled=True),
        lax.all_to_all(slot_gate, "exp", split_axis=0, concat_axis=0, tiled=True),
    )
    rows_all, gate_all = (
        lax.all_gather(rows_in, "seq", axis=0, tiled=True),
        lax.all_gather(gate_in, "seq", axis=0, tiled=True),
    )
    halves = seq_count // EXP_COL
    expert_pick = lax.axis_index("seq") // halves
    flat_rows = rows_all.reshape(-1, model_width)
    flat_gate = lax.dynamic_index_in_dim(
        gate_all.reshape(-1, EXP_COL), expert_pick, axis=1, keepdims=False
    )
    gate_block = w_gate[0, 0]
    up_block = w_up[0, 0]
    down_block = w_down[0, 0]
    gate_proj = jnp.dot(flat_rows, gate_block, preferred_element_type=jnp.float32)
    up_proj = jnp.dot(flat_rows, up_block, preferred_element_type=jnp.float32)
    activated = (jax.nn.silu(gate_proj) * up_proj).astype(jnp.bfloat16)
    partial_value = jnp.dot(activated, down_block, preferred_element_type=jnp.float32).astype(
        jnp.bfloat16
    )
    partial_value = lax.optimization_barrier(partial_value)
    node_sum = lax.psum_scatter(
        (partial_value.astype(jnp.float32) * flat_gate.astype(jnp.float32)[:, None]).astype(
            jnp.bfloat16
        ),
        "seq",
        scatter_dimension=0,
        tiled=True,
    )
    gathered_output = lax.all_to_all(
        node_sum.reshape(columns, capacity, model_width),
        "exp",
        split_axis=0,
        concat_axis=0,
        tiled=True,
    )
    mixture_expert_total = jnp.einsum(
        "gyr,yre->ge", slot_flag_mask, gathered_output, preferred_element_type=jnp.float32
    )
    return (hidden + mixture_expert_total).astype(jnp.bfloat16)[None]

CORE, X_BIT, Y_BIT = 1, 2, 4
CHUNKS = 2


def exchange(value, mask):
    columns = lax.axis_size("exp")
    return lax.ppermute(value, "exp", [(i, i ^ mask) for i in range(columns)])


def shift(value, step):
    seq_count = lax.axis_size("seq")
    return lax.ppermute(value, "seq", [(i, (i + step) % seq_count) for i in range(seq_count)])


def add_rounded(first, second):
    return (first.astype(jnp.float32) + second.astype(jnp.float32)).astype(jnp.bfloat16)


def attend_at(query_rows, key_rows, value_rows, position, length_row):
    row_count = query_rows.shape[0]
    groups = key_rows.shape[1] // HEAD_DIM
    per_group = query_rows.shape[1] // HEAD_DIM // groups
    bounds = jnp.cumsum(length_row)
    episode = jnp.sum((position[:, None] >= bounds[None, :]).astype(jnp.int32), axis=1)
    q_heads = query_rows.reshape(row_count, groups, per_group, HEAD_DIM)
    k_heads = key_rows.reshape(row_count, groups, HEAD_DIM)
    v_heads = value_rows.reshape(row_count, groups, HEAD_DIM)
    scores = jnp.einsum(
        "tgpd,ugd->gptu", q_heads, k_heads, preferred_element_type=jnp.float32
    ) / math.sqrt(HEAD_DIM)
    allowed = (episode[:, None] == episode[None, :]) & (position[None, :] <= position[:, None])
    scores = jnp.where(allowed, scores, -jnp.inf)
    row_maximum = jnp.max(scores, axis=-1, keepdims=True)
    weights = jnp.exp(scores - row_maximum)
    probability = (weights / jnp.sum(weights, axis=-1, keepdims=True)).astype(jnp.bfloat16)
    mixed = jnp.einsum("gptu,ugd->tgpd", probability, v_heads, preferred_element_type=jnp.float32)
    return mixed.astype(jnp.bfloat16).reshape(row_count, groups * per_group * HEAD_DIM)


def project(mixed, out_weight, token_count):
    seq_count = lax.axis_size("seq")
    columns = lax.axis_size("exp")
    width = out_weight.shape[1] // 2
    own = (out_weight[:, :width], out_weight[:, width:])
    pieces = {}
    for half, (first, second) in enumerate(((X_BIT, Y_BIT), (Y_BIT, X_BIT))):
        pieces[half, 0] = own[half]
        pieces[half, first] = exchange(own[half], first)
        pieces[half, second] = exchange(own[half], second)
        pieces[half, first | second] = exchange(pieces[half, first], second)
    for half, m in list(pieces):
        pieces[half, m | CORE] = exchange(pieces[half, m], CORE)
    groups = (
        [(h, m) for h in range(2) for m in (0, 1)],
        [(0, X_BIT), (0, X_BIT | 1), (1, Y_BIT), (1, Y_BIT | 1)],
        [(0, Y_BIT), (0, Y_BIT | 1), (1, X_BIT), (1, X_BIT | 1)],
        [(h, m) for h in range(2) for m in (6, 7)],
    )
    reduced = {}
    for names in groups:
        weight = jnp.concatenate([pieces[name] for name in names], axis=1)
        part = jnp.dot(mixed, weight, preferred_element_type=jnp.float32).astype(jnp.bfloat16)
        total = part[:token_count].astype(jnp.float32)
        for k in range(1, seq_count):
            total = total + shift(part[k * token_count : (k + 1) * token_count], -k).astype(
                jnp.float32
            )
        for place, name in enumerate(names):
            reduced[name] = total[:, place * width : (place + 1) * width]
    halves = [jnp.stack([reduced[h, m] for m in range(columns)]) for h in range(2)]
    here = lax.axis_index("exp")
    in_order = []
    for c in range(columns):
        for h in range(2):
            in_order.append(lax.dynamic_index_in_dim(halves[h], here ^ c, 0, keepdims=False))
    return jnp.concatenate(in_order, axis=1)


def gather_gates(node_gate):
    seq_count = lax.axis_size("seq")
    value = jnp.stack([node_gate] + [shift(node_gate, k) for k in range(1, seq_count)])
    for mask in (X_BIT, Y_BIT, CORE):
        value = jnp.stack([value, exchange(value, mask)])
    pick = lax.axis_index("exp") * EXP_COL + lax.axis_index("seq") // (seq_count // EXP_COL)
    return lax.dynamic_index_in_dim(value, pick, axis=value.ndim - 1, keepdims=False)


FAR_ORDER = ((X_BIT, Y_BIT), (Y_BIT, X_BIT))
PLACES = (0, X_BIT, Y_BIT, X_BIT | Y_BIT)
together = lax.optimization_barrier


def spread_seq(rows):
    seq_count = lax.axis_size("seq")
    blocks = [rows] + [shift(rows, k) for k in range(1, seq_count)]
    near = seq_count // 2
    return [jnp.concatenate(blocks[h * near : (h + 1) * near], axis=0) for h in range(2)]


def spread_once(halves):
    return [
        {0: own, first: exchange(own, first), second: exchange(own, second)}
        for own, (first, second) in zip(halves, FAR_ORDER)
    ]


def spread_twice(held):
    return [
        {**part, first | second: exchange(part[first], second)}
        for part, (first, second) in zip(held, FAR_ORDER)
    ]


def same_parity(held):
    return jnp.concatenate([part[m] for part in held for m in PLACES], axis=0)


def collect_once(summed):
    size = summed.shape[0] // 8
    held = []
    for half, (first, second) in enumerate(FAR_ORDER):
        part = {}
        for place, m in enumerate(PLACES):
            start = (4 * half + place) * size
            part[m] = summed[start : start + size]
        got_far = exchange(part[first | second], second)
        got_near = exchange(part[second], second)
        held.append((part[0], part[first], got_far, got_near))
    return held


def collect_twice(held):
    done = []
    for (own, onward, got_far, got_near), (first, _) in zip(held, FAR_ORDER):
        got = exchange(add_rounded(onward, got_far), first)
        done.append((own, got_near, got))
    return done


def collect_seq(done, row_count):
    seq_count = lax.axis_size("seq")
    near = seq_count // 2
    total = None
    for half, terms in enumerate(done):
        mine = sum(term.astype(jnp.float32) for term in terms).astype(jnp.bfloat16)
        for j in range(near):
            k = half * near + j
            block = mine[j * row_count : (j + 1) * row_count]
            block = block if k == 0 else shift(block, -k)
            block = block.astype(jnp.float32)
            total = block if total is None else total + block
    return total


def activate(gate_proj, rows, scale, w_up):
    up_proj = jnp.dot(rows, w_up, preferred_element_type=jnp.float32)
    return (jax.nn.silu(gate_proj) * up_proj * scale.astype(jnp.float32)).astype(jnp.bfloat16)


def local_dense(
    queries,
    key_heads,
    value_heads,
    residual,
    lengths,
    routes,
    gate_weights,
    out_weight,
    norm_gain,
    w_gate,
    w_up,
    w_down,
):
    seq_count = lax.axis_size("seq")
    columns = lax.axis_size("exp")
    token_count = residual.shape[1]
    place = lax.axis_index("seq")

    def heads_of(k):
        owner = lax.rem(place + k, seq_count)
        parts = []
        for whole in (queries[0], key_heads[0], value_heads[0]):
            width = whole.shape[1] // seq_count
            parts.append(lax.dynamic_slice_in_dim(whole, owner * width, width, axis=1))
        return jnp.concatenate(parts, axis=1)

    arrived = [heads_of(0)] + [shift(heads_of(k), k) for k in range(1, seq_count)]
    rows = jnp.concatenate(arrived, axis=0)
    q_width = queries.shape[2] // seq_count
    k_width = key_heads.shape[2] // seq_count
    position = jnp.concatenate(
        [
            lax.rem(place - k + seq_count, seq_count) * token_count
            + jnp.arange(token_count, dtype=jnp.int32)
            for k in range(seq_count)
        ]
    )
    mixed = attend_at(
        rows[:, :q_width],
        rows[:, q_width : q_width + k_width],
        rows[:, q_width + k_width :],
        position,
        lengths[0],
    )

    routed = routes[0]
    node_count = routed.shape[1]
    on_node = routed[:, :, None] == jnp.arange(columns, dtype=jnp.int32)[None, None, :]
    gate_pair = gate_weights[0].reshape(token_count, node_count, EXP_COL).astype(jnp.float32)
    node_gate = jnp.sum(jnp.where(on_node[:, :, :, None], gate_pair[:, :, None, :], 0.0), axis=1)
    node_gate = node_gate.astype(jnp.bfloat16).reshape(token_count, columns * EXP_COL)
    gates = gather_gates(node_gate)

    hidden = residual[0].astype(jnp.float32) + project(mixed, out_weight, token_count)
    inverse = lax.rsqrt(jnp.mean(hidden * hidden, axis=1, keepdims=True) + epsilon)
    normalized_rows = (hidden * inverse * norm_gain[None, :]).astype(jnp.bfloat16)

    row_count = token_count // CHUNKS
    near = seq_count // 2
    gates = gates.reshape(2, 2, 2, 2, near, CHUNKS, row_count)
    gates = jnp.transpose(gates, (5, 0, 3, 1, 2, 4, 6)).reshape(CHUNKS, -1)
    gate_block, up_block, down_block = w_gate[0, 0], w_up[0, 0], w_down[0, 0]
    scales = [
        jnp.broadcast_to(gates[c][:, None], (gates.shape[1], up_block.shape[1]))
        for c in range(CHUNKS)
    ]
    normalized_rows, scales = together((normalized_rows, scales))

    def dot_gate(rows):
        return jnp.dot(rows, gate_block, preferred_element_type=jnp.float32)

    def dot_down(activated):
        return jnp.dot(activated, down_block, preferred_element_type=jnp.float32).astype(
            jnp.bfloat16
        )

    ahead = spread_seq(normalized_rows[:row_count])
    behind = spread_seq(normalized_rows[row_count:])
    same = same_parity(spread_twice(spread_once(ahead)))
    rows = jnp.concatenate([same, exchange(same, CORE)], axis=0)
    rows, behind = together((rows, behind))
    held = spread_once(behind)
    gate_proj = dot_gate(rows)
    held, gate_proj = together((held, gate_proj))
    held = spread_twice(held)
    activated = activate(gate_proj, rows, scales[0], up_block)
    held, activated = together((held, activated))
    same = same_parity(held)
    other = exchange(same, CORE)
    part = dot_down(activated)
    same, other, part = together((same, other, part))
    size = part.shape[0] // 2
    crossing = exchange(part[size:], CORE)
    rows = jnp.concatenate([same, other], axis=0)
    gate_proj = dot_gate(rows)
    crossing, gate_proj = together((crossing, gate_proj))
    returned = collect_once(add_rounded(part[:size], crossing))
    activated = activate(gate_proj, rows, scales[1], up_block)
    returned, activated = together((returned, activated))
    returned = collect_twice(returned)
    part = dot_down(activated)
    returned, part = together((returned, part))
    first_total = collect_seq(returned, row_count)
    returned = collect_once(add_rounded(part[:size], exchange(part[size:], CORE)))
    second_total = collect_seq(collect_twice(returned), row_count)
    total = jnp.concatenate([first_total, second_total], axis=0)
    return (hidden + total).astype(jnp.bfloat16)[None]


def solution(mesh):
    cube = (CORE | X_BIT | Y_BIT) + 1
    dense = mesh.shape["exp"] == cube and mesh.shape["seq"] % 2 == 0
    return jax.shard_map(
        local_dense if dense else local_routed,
        mesh=mesh,
        in_specs=(
            P("exp", "seq", None),
            P("exp", "seq", None),
            P("exp", "seq", None),
            P("exp", "seq", None),
            P("exp", None),
            P("exp", "seq", None),
            P("exp", "seq", None),
            P("seq", "exp"),
            P(),
            P("exp", "seq", None, None),
            P("exp", "seq", None, None),
            P("exp", "seq", None, None),
        ),
        out_specs=P("exp", "seq", None),
        check_vma=False,
    )
```

```python
import math

import jax
import jax.numpy as jnp
from jax import lax
from jax.sharding import PartitionSpec as P

HEAD_DIM = 128
EXP_COL = 2


epsilon = 1e-06


def episode_ids(length_row, position_count):
    bounds = jnp.cumsum(length_row)
    position = jnp.arange(position_count, dtype=jnp.int32)
    return jnp.sum((position[:, None] >= bounds[None, :]).astype(jnp.int32), axis=1)


def attend(query_rows, key_rows, value_rows, episode):
    row_count = query_rows.shape[0]
    groups = key_rows.shape[1] // HEAD_DIM
    per_group = query_rows.shape[1] // HEAD_DIM // groups
    q_heads = query_rows.reshape(row_count, groups, per_group, HEAD_DIM)
    k_heads = key_rows.reshape(row_count, groups, HEAD_DIM)
    v_heads = value_rows.reshape(row_count, groups, HEAD_DIM)
    scores = jnp.einsum(
        "tgpd,ugd->gptu", q_heads, k_heads, preferred_element_type=jnp.float32
    ) / math.sqrt(HEAD_DIM)
    position = jnp.arange(row_count, dtype=jnp.int32)
    allowed = (episode[:, None] == episode[None, :]) & (position[None, :] <= position[:, None])
    scores = jnp.where(allowed, scores, -jnp.inf)
    row_maximum = jnp.max(scores, axis=-1, keepdims=True)
    weights = jnp.exp(scores - row_maximum)
    probability = (weights / jnp.sum(weights, axis=-1, keepdims=True)).astype(jnp.bfloat16)
    mixed = jnp.einsum("gptu,ugd->tgpd", probability, v_heads, preferred_element_type=jnp.float32)
    return mixed.astype(jnp.bfloat16).reshape(row_count, groups * per_group * HEAD_DIM)


def local_routed(
    queries,
    key_heads,
    value_heads,
    residual,
    lengths,
    routes,
    gate_weights,
    out_weight,
    norm_gain,
    w_gate,
    w_up,
    w_down,
):
    seq_count = lax.axis_size("seq")
    columns = lax.axis_size("exp")
    token_count = residual.shape[1]
    model_width = residual.shape[2]
    whole_q, whole_k, whole_v = (
        lax.all_to_all(queries[0], "seq", split_axis=1, concat_axis=0, tiled=True),
        lax.all_to_all(key_heads[0], "seq", split_axis=1, concat_axis=0, tiled=True),
        lax.all_to_all(value_heads[0], "seq", split_axis=1, concat_axis=0, tiled=True),
    )
    episode = episode_ids(lengths[0], whole_q.shape[0])
    mixed = attend(whole_q, whole_k, whole_v, episode)
    head_partial = jnp.dot(
        mixed,
        lax.all_gather(out_weight, "exp", axis=1, tiled=True),
        preferred_element_type=jnp.float32,
    )
    projected = lax.psum_scatter(
        head_partial.astype(jnp.bfloat16), "seq", scatter_dimension=0, tiled=True
    ).astype(jnp.float32)
    hidden = residual[0].astype(jnp.float32) + projected
    inverse = lax.rsqrt(jnp.mean(hidden * hidden, axis=1, keepdims=True) + epsilon)
    normalized_rows = (hidden * inverse * norm_gain[None, :]).astype(jnp.bfloat16)
    routed = routes[0]
    node_count = routed.shape[1]
    capacity = max(2, 5 * token_count * node_count // (4 * columns))
    on_node = routed[:, :, None] == jnp.arange(columns, dtype=jnp.int32)[None, None, :]
    member = jnp.sum(on_node.astype(jnp.int32), axis=1)
    before = jnp.cumsum(member, axis=0) - member
    slot_lookup_index = (
        before[:, :, None] == jnp.arange(capacity, dtype=jnp.int32)[None, None, :]
    ) & (member[:, :, None] > 0)
    slot_flag_mask = slot_lookup_index.astype(jnp.bfloat16)
    outbound = jnp.einsum(
        "roj,rm->ojm", slot_flag_mask, normalized_rows, preferred_element_type=jnp.float32
    ).astype(jnp.bfloat16)
    gate_pair = gate_weights[0].reshape(token_count, node_count, EXP_COL).astype(jnp.float32)
    node_route_gate = jnp.einsum(
        "tnc,tne->tce", on_node.astype(jnp.float32), gate_pair, precision=lax.Precision.HIGHEST
    )
    slot_gate = jnp.einsum(
        "qnr,qny->nry",
        slot_lookup_index.astype(jnp.float32),
        node_route_gate,
        precision=lax.Precision.HIGHEST,
    ).astype(jnp.bfloat16)
    rows_in, gate_in = (
        lax.all_to_all(outbound, "exp", split_axis=0, concat_axis=0, tiled=True),
        lax.all_to_all(slot_gate, "exp", split_axis=0, concat_axis=0, tiled=True),
    )
    rows_all, gate_all = (
        lax.all_gather(rows_in, "seq", axis=0, tiled=True),
        lax.all_gather(gate_in, "seq", axis=0, tiled=True),
    )
    halves = seq_count // EXP_COL
    expert_pick = lax.axis_index("seq") // halves
    flat_rows = rows_all.reshape(-1, model_width)
    flat_gate = lax.dynamic_index_in_dim(
        gate_all.reshape(-1, EXP_COL), expert_pick, axis=1, keepdims=False
    )
    gate_block = w_gate[0, 0]
    up_block = w_up[0, 0]
    down_block = w_down[0, 0]
    gate_proj = jnp.dot(flat_rows, gate_block, preferred_element_type=jnp.float32)
    up_proj = jnp.dot(flat_rows, up_block, preferred_element_type=jnp.float32)
    activated = (jax.nn.silu(gate_proj) * up_proj).astype(jnp.bfloat16)
    partial_value = jnp.dot(activated, down_block, preferred_element_type=jnp.float32).astype(
        jnp.bfloat16
    )
    partial_value = lax.optimization_barrier(partial_value)
    node_sum = lax.psum_scatter(
        (partial_value.astype(jnp.float32) * flat_gate.astype(jnp.float32)[:, None]).astype(
            jnp.bfloat16
        ),
        "seq",
        scatter_dimension=0,
        tiled=True,
    )
    gathered_output = lax.all_to_all(
        node_sum.reshape(columns, capacity, model_width),
        "exp",
        split_axis=0,
        concat_axis=0,
        tiled=True,
    )
    mixture_expert_total = jnp.einsum(
        "gyr,yre->ge", slot_flag_mask, gathered_output, preferred_element_type=jnp.float32
    )
    return (hidden + mixture_expert_total).astype(jnp.bfloat16)[None]

CORE, X_BIT, Y_BIT = 1, 2, 4
CHUNKS = 2


def exchange(value, mask):
    columns = lax.axis_size("exp")
    return lax.ppermute(value, "exp", [(i, i ^ mask) for i in range(columns)])


def shift(value, step):
    seq_count = lax.axis_size("seq")
    return lax.ppermute(value, "seq", [(i, (i + step) % seq_count) for i in range(seq_count)])


def add_rounded(first, second):
    return (first.astype(jnp.float32) + second.astype(jnp.float32)).astype(jnp.bfloat16)


def attend_at(query_rows, key_rows, value_rows, position, length_row):
    row_count = query_rows.shape[0]
    groups = key_rows.shape[1] // HEAD_DIM
    per_group = query_rows.shape[1] // HEAD_DIM // groups
    bounds = jnp.cumsum(length_row)
    episode = jnp.sum((position[:, None] >= bounds[None, :]).astype(jnp.int32), axis=1)
    q_heads = query_rows.reshape(row_count, groups, per_group, HEAD_DIM)
    k_heads = key_rows.reshape(row_count, groups, HEAD_DIM)
    v_heads = value_rows.reshape(row_count, groups, HEAD_DIM)
    scores = jnp.einsum(
        "tgpd,ugd->gptu", q_heads, k_heads, preferred_element_type=jnp.float32
    ) / math.sqrt(HEAD_DIM)
    allowed = (episode[:, None] == episode[None, :]) & (position[None, :] <= position[:, None])
    scores = jnp.where(allowed, scores, -jnp.inf)
    row_maximum = jnp.max(scores, axis=-1, keepdims=True)
    weights = jnp.exp(scores - row_maximum)
    probability = (weights / jnp.sum(weights, axis=-1, keepdims=True)).astype(jnp.bfloat16)
    mixed = jnp.einsum("gptu,ugd->tgpd", probability, v_heads, preferred_element_type=jnp.float32)
    return mixed.astype(jnp.bfloat16).reshape(row_count, groups * per_group * HEAD_DIM)


def project(mixed, out_weight, token_count):
    seq_count = lax.axis_size("seq")
    columns = lax.axis_size("exp")
    width = out_weight.shape[1] // 2
    own = (out_weight[:, :width], out_weight[:, width:])
    pieces = {}
    for half, (first, second) in enumerate(((X_BIT, Y_BIT), (Y_BIT, X_BIT))):
        pieces[half, 0] = own[half]
        pieces[half, first] = exchange(own[half], first)
        pieces[half, second] = exchange(own[half], second)
        pieces[half, first | second] = exchange(pieces[half, first], second)
    for half, m in list(pieces):
        pieces[half, m | CORE] = exchange(pieces[half, m], CORE)
    groups = (
        [(h, m) for h in range(2) for m in (0, 1)],
        [(0, X_BIT), (0, X_BIT | 1), (1, Y_BIT), (1, Y_BIT | 1)],
        [(0, Y_BIT), (0, Y_BIT | 1), (1, X_BIT), (1, X_BIT | 1)],
        [(h, m) for h in range(2) for m in (6, 7)],
    )
    reduced = {}
    for names in groups:
        weight = jnp.concatenate([pieces[name] for name in names], axis=1)
        part = jnp.dot(mixed, weight, preferred_element_type=jnp.float32).astype(jnp.bfloat16)
        total = part[:token_count].astype(jnp.float32)
        for k in range(1, seq_count):
            total = total + shift(part[k * token_count : (k + 1) * token_count], -k).astype(
                jnp.float32
            )
        for place, name in enumerate(names):
            reduced[name] = total[:, place * width : (place + 1) * width]
    halves = [jnp.stack([reduced[h, m] for m in range(columns)]) for h in range(2)]
    here = lax.axis_index("exp")
    in_order = []
    for c in range(columns):
        for h in range(2):
            in_order.append(lax.dynamic_index_in_dim(halves[h], here ^ c, 0, keepdims=False))
    return jnp.concatenate(in_order, axis=1)


def gather_gates(node_gate):
    seq_count = lax.axis_size("seq")
    value = jnp.stack([node_gate] + [shift(node_gate, k) for k in range(1, seq_count)])
    for mask in (X_BIT, Y_BIT, CORE):
        value = jnp.stack([value, exchange(value, mask)])
    pick = lax.axis_index("exp") * EXP_COL + lax.axis_index("seq") // (seq_count // EXP_COL)
    return lax.dynamic_index_in_dim(value, pick, axis=value.ndim - 1, keepdims=False)


FAR_ORDER = ((X_BIT, Y_BIT), (Y_BIT, X_BIT))
PLACES = (0, X_BIT, Y_BIT, X_BIT | Y_BIT)
together = lax.optimization_barrier


def spread_seq(rows):
    seq_count = lax.axis_size("seq")
    blocks = [rows] + [shift(rows, k) for k in range(1, seq_count)]
    near = seq_count // 2
    return [jnp.concatenate(blocks[h * near : (h + 1) * near], axis=0) for h in range(2)]


def spread_once(halves):
    return [
        {0: own, first: exchange(own, first), second: exchange(own, second)}
        for own, (first, second) in zip(halves, FAR_ORDER)
    ]


def spread_twice(held):
    return [
        {**part, first | second: exchange(part[first], second)}
        for part, (first, second) in zip(held, FAR_ORDER)
    ]


def same_parity(held):
    return jnp.concatenate([part[m] for part in held for m in PLACES], axis=0)


def collect_once(summed):
    size = summed.shape[0] // 8
    held = []
    for half, (first, second) in enumerate(FAR_ORDER):
        part = {}
        for place, m in enumerate(PLACES):
            start = (4 * half + place) * size
            part[m] = summed[start : start + size]
        got_far = exchange(part[first | second], second)
        got_near = exchange(part[second], second)
        held.append((part[0], part[first], got_far, got_near))
    return held


def collect_twice(held):
    done = []
    for (own, onward, got_far, got_near), (first, _) in zip(held, FAR_ORDER):
        got = exchange(add_rounded(onward, got_far), first)
        done.append((own, got_near, got))
    return done


def collect_seq(done, row_count):
    seq_count = lax.axis_size("seq")
    near = seq_count // 2
    total = None
    for half, terms in enumerate(done):
        mine = sum(term.astype(jnp.float32) for term in terms).astype(jnp.bfloat16)
        for j in range(near):
            k = half * near + j
            block = mine[j * row_count : (j + 1) * row_count]
            block = block if k == 0 else shift(block, -k)
            block = block.astype(jnp.float32)
            total = block if total is None else total + block
    return total


def activate(gate_proj, rows, scale, w_up):
    up_proj = jnp.dot(rows, w_up, preferred_element_type=jnp.float32)
    return (jax.nn.silu(gate_proj) * up_proj * scale.astype(jnp.float32)).astype(jnp.bfloat16)


def local_dense(
    queries,
    key_heads,
    value_heads,
    residual,
    lengths,
    routes,
    gate_weights,
    out_weight,
    norm_gain,
    w_gate,
    w_up,
    w_down,
):
    seq_count = lax.axis_size("seq")
    columns = lax.axis_size("exp")
    token_count = residual.shape[1]
    place = lax.axis_index("seq")

    def heads_of(k):
        owner = lax.rem(place + k, seq_count)
        parts = []
        for whole in (queries[0], key_heads[0], value_heads[0]):
            width = whole.shape[1] // seq_count
            parts.append(lax.dynamic_slice_in_dim(whole, owner * width, width, axis=1))
        return jnp.concatenate(parts, axis=1)

    arrived = [heads_of(0)] + [shift(heads_of(k), k) for k in range(1, seq_count)]
    rows = jnp.concatenate(arrived, axis=0)
    q_width = queries.shape[2] // seq_count
    k_width = key_heads.shape[2] // seq_count
    position = jnp.concatenate(
        [
            lax.rem(place - k + seq_count, seq_count) * token_count
            + jnp.arange(token_count, dtype=jnp.int32)
            for k in range(seq_count)
        ]
    )
    mixed = attend_at(
        rows[:, :q_width],
        rows[:, q_width : q_width + k_width],
        rows[:, q_width + k_width :],
        position,
        lengths[0],
    )

    routed = routes[0]
    node_count = routed.shape[1]
    on_node = routed[:, :, None] == jnp.arange(columns, dtype=jnp.int32)[None, None, :]
    gate_pair = gate_weights[0].reshape(token_count, node_count, EXP_COL).astype(jnp.float32)
    node_gate = jnp.sum(jnp.where(on_node[:, :, :, None], gate_pair[:, :, None, :], 0.0), axis=1)
    node_gate = node_gate.astype(jnp.bfloat16).reshape(token_count, columns * EXP_COL)
    gates = gather_gates(node_gate)

    hidden = residual[0].astype(jnp.float32) + project(mixed, out_weight, token_count)
    inverse = lax.rsqrt(jnp.mean(hidden * hidden, axis=1, keepdims=True) + epsilon)
    normalized_rows = (hidden * inverse * norm_gain[None, :]).astype(jnp.bfloat16)

    row_count = token_count // CHUNKS
    near = seq_count // 2
    gates = gates.reshape(2, 2, 2, 2, near, CHUNKS, row_count)
    gates = jnp.transpose(gates, (5, 0, 3, 1, 2, 4, 6)).reshape(CHUNKS, -1)
    gate_block, up_block, down_block = w_gate[0, 0], w_up[0, 0], w_down[0, 0]
    scales = [
        jnp.broadcast_to(gates[c][:, None], (gates.shape[1], up_block.shape[1]))
        for c in range(CHUNKS)
    ]
    normalized_rows, scales = together((normalized_rows, scales))

    def dot_gate(rows):
        return jnp.dot(rows, gate_block, preferred_element_type=jnp.float32)

    def dot_down(activated):
        return jnp.dot(activated, down_block, preferred_element_type=jnp.float32).astype(
            jnp.bfloat16
        )

    ahead = spread_seq(normalized_rows[:row_count])
    ahead, late_rows = together((ahead, normalized_rows[row_count:]))
    behind = spread_seq(late_rows)
    held, behind = together((spread_twice(spread_once(ahead)), behind))
    same = same_parity(held)
    rows = jnp.concatenate([same, exchange(same, CORE)], axis=0)
    rows, behind = together((rows, behind))
    held = spread_once(behind)
    gate_proj = dot_gate(rows)
    held, gate_proj = together((held, gate_proj))
    held = spread_twice(held)
    activated = activate(gate_proj, rows, scales[0], up_block)
    held, activated = together((held, activated))
    same = same_parity(held)
    other = exchange(same, CORE)
    part = dot_down(activated)
    same, other, part = together((same, other, part))
    size = part.shape[0] // 2
    crossing = exchange(part[size:], CORE)
    rows = jnp.concatenate([same, other], axis=0)
    gate_proj = dot_gate(rows)
    crossing, gate_proj = together((crossing, gate_proj))
    returned = collect_once(add_rounded(part[:size], crossing))
    activated = activate(gate_proj, rows, scales[1], up_block)
    returned, activated = together((returned, activated))
    returned = collect_twice(returned)
    part = dot_down(activated)
    returned, part = together((returned, part))
    first_total = collect_seq(returned, row_count)
    returned = collect_once(add_rounded(part[:size], exchange(part[size:], CORE)))
    returned, first_total = together((returned, first_total))
    second_total = collect_seq(collect_twice(returned), row_count)
    total = jnp.concatenate([first_total, second_total], axis=0)
    return (hidden + total).astype(jnp.bfloat16)[None]


def solution(mesh):
    cube = (CORE | X_BIT | Y_BIT) + 1
    dense = mesh.shape["exp"] == cube and mesh.shape["seq"] % 2 == 0
    return jax.shard_map(
        local_dense if dense else local_routed,
        mesh=mesh,
        in_specs=(
            P("exp", "seq", None),
            P("exp", "seq", None),
            P("exp", "seq", None),
            P("exp", "seq", None),
            P("exp", None),
            P("exp", "seq", None),
            P("exp", "seq", None),
            P("seq", "exp"),
            P(),
            P("exp", "seq", None, None),
            P("exp", "seq", None, None),
            P("exp", "seq", None, None),
        ),
        out_specs=P("exp", "seq", None),
        check_vma=False,
    )
```
